32 devices in a mesh: dp: 4 (over x, core), fsdp: 8 (over z, y).
Axes of the slice: x: 2, y: 2, z: 4, core: 2. Of those that a mesh axis runs over, the one named last changes fastest.
Arguments:
- tokens: bfloat16 [2, 32, 256, 1024], P(None, None, ('dp', 'fsdp')), may hold values from -6 to 6
- lengths: int32 [2, 32], replicated, may hold values from 1 to 256, 5120 in all within a row
- deal_order: int32 [2, 32], replicated, may hold values from 0 to 31, each once within a row
- decay_rates: float32 [8], replicated, may hold values from 0.0001 to 0.03
- query_weight: bfloat16 [1024, 1024], P(('dp', 'fsdp')), may hold values from -0.1875 to 0.1875
- key_weight: bfloat16 [1024, 1024], P(('dp', 'fsdp')), may hold values from -0.1875 to 0.1875
- value_weight: bfloat16 [1024, 1024], P(('dp', 'fsdp')), may hold values from -0.1875 to 0.1875
- gate_weight: bfloat16 [1024, 1024], P(('dp', 'fsdp')), may hold values from -0.1875 to 0.1875
- out_weight: bfloat16 [1024, 1024], P(('dp', 'fsdp')), may hold values from -0.1875 to 0.1875
- glu_left: bfloat16 [1024, 2816], P(('dp', 'fsdp')), may hold values from -0.1875 to 0.1875
- glu_right: bfloat16 [1024, 2816], P(('dp', 'fsdp')), may hold values from -0.1875 to 0.1875
- glu_down: bfloat16 [2816, 1024], P(('dp', 'fsdp')), may hold values from -0.109375 to 0.109375
- cotangent: bfloat16 [2, 32, 256, 1024], P(None, ('dp', 'fsdp')), may hold values from -6 to 6
Outputs:
- layer_output: bfloat16 [2, 32, 256, 1024], P(None, None, ('dp', 'fsdp'))
- input_grad: bfloat16 [2, 32, 256, 1024], P(None, None, ('dp', 'fsdp'))
- query_grad: float32 [1024, 1024], P(('dp', 'fsdp'))
- key_grad: float32 [1024, 1024], P(('dp', 'fsdp'))
- value_grad: float32 [1024, 1024], P(('dp', 'fsdp'))
- gate_grad: float32 [1024, 1024], P(('dp', 'fsdp'))
- out_grad: float32 [1024, 1024], P(('dp', 'fsdp'))
- left_grad: float32 [1024, 2816], P(('dp', 'fsdp'))
- right_grad: float32 [1024, 2816], P(('dp', 'fsdp'))
- down_grad: float32 [2816, 1024], P(('dp', 'fsdp'))
The draws below stay inside these ranges and needn't reach their ends.
Inputs may be any that keep to these rules, and one draw needn't show every extreme that they name: `deal_order`: each micro-batch's row names every one of the 32 sequences exactly once. Each micro-batch's lengths add up to 5120, and the longest equals 256.
All inputs are finite; a program needn't handle non-finite values.
Results may differ from the reference program's by a relative error of at most 0.014.
Values may be sent and summed in bfloat16 or wider, within the bound.
A program may use at most 192 MiB of HBM per device.

```python
import math
import jax
import jax.numpy as jnp
import numpy as np
from jax import lax

D = 1024
HEADS = 8
HDIM = 128
FF = 2816
LMAX = 256
MB = 2
SEQS = 32


def block_scale(key, dims, pieces, low, high):
    gain, own = 1.0, jax.random.fold_in(key, 6)
    for axis_at, blocks in pieces:
        heights = jnp.exp(jax.random.uniform(jax.random.fold_in(own, axis_at), (blocks,), jnp.float32, low / len(pieces), high / len(pieces)))
        gain = gain * jnp.repeat(heights, dims[axis_at] // blocks).reshape([-1 if axis == axis_at else 1 for axis in range(len(dims))])
    return gain


def length_profile(number_of, total, most, lean):
    weights = [(1 << 20) // math.isqrt(standing ** lean) + 1 for standing in range(2, number_of + 1)]
    rest, given = total - most - (number_of - 1), [1] * (number_of - 1)
    while rest > 0:
        movable = [i for i in range(number_of - 1) if given[i] < most]
        mass, budget = sum([weights[i] for i in movable]), rest
        for i in movable:
            addition = min(most - given[i], max(1, budget * weights[i] // mass), rest)
            given[i] = given[i] + addition
            rest = rest - addition
    return np.array([most] + given)


def ragged_sizes(key, count, total, reach, slope):
    if count == 2:
        one = jax.random.randint(key, (), max(1, total - reach), min(reach, total - 1) + 1)
        return jnp.stack([one, total - one])
    tallies = jnp.asarray(length_profile(count, total, reach, slope), jnp.int32)
    pairs = (count - 1) // 2
    source_of, taker = tallies[1:1 + 2 * pairs:2], tallies[2:2 + 2 * pairs:2]
    margin = jnp.minimum(source_of - 1, reach - taker)
    moved = jax.random.randint(jax.random.fold_in(key, 1), (pairs,), 0, 1 << 20) % (margin + 1)
    tallies = tallies.at[1:1 + 2 * pairs:2].set(source_of - moved).at[2:2 + 2 * pairs:2].set(taker + moved)
    return tallies[jax.random.permutation(jax.random.fold_in(key, 2), count)]


def normal_values(own_key, shape, width, limit, split=(), held_as=jnp.bfloat16):
    array = width * jax.random.normal(own_key, shape, jnp.float32)
    if split:
        array = array * block_scale(own_key, shape, split, -0.22, 0.18)
    return jnp.clip(array, -limit, limit).astype(held_as)


def setup_inputs(seed: int = 0) -> dict:
    splits = jax.random.split(jax.random.key(seed), 14)
    return {
        "tokens": normal_values(splits[0], (MB, SEQS, LMAX, D), 1.0, 6.0, ((2, 32),)),
        "lengths": jax.vmap(lambda own: ragged_sizes(own, SEQS, 5 * SEQS * LMAX // 8, LMAX, 1))(jax.random.split(splits[1], MB)).reshape((MB, SEQS)).astype(jnp.int32),
        "deal_order": jax.vmap(lambda own: jax.random.permutation(own, SEQS))(jax.random.split(splits[2], MB)).reshape((MB, SEQS)).astype(jnp.int32),
        "decay_rates": jnp.clip(jnp.exp(jax.random.uniform(splits[3], (HEADS,), jnp.float32, math.log(0.0001), math.log(0.03))), 0.0001, 0.03),
        "query_weight": normal_values(splits[4], (D, D), D ** -0.5, 0.1875, ((0, 32),)),
        "key_weight": normal_values(splits[5], (D, D), D ** -0.5, 0.1875, ((0, 32),)),
        "value_weight": normal_values(splits[6], (D, D), D ** -0.5, 0.1875, ((0, 32),)),
        "gate_weight": normal_values(splits[7], (D, D), D ** -0.5, 0.1875, ((0, 32),)),
        "out_weight": normal_values(splits[8], (D, D), D ** -0.5, 0.1875, ((0, 32),)),
        "glu_left": normal_values(splits[9], (D, FF), D ** -0.5, 0.1875, ((0, 32),)),
        "glu_right": normal_values(splits[10], (D, FF), D ** -0.5, 0.1875, ((0, 32),)),
        "glu_down": normal_values(splits[11], (FF, D), FF ** -0.5, 0.109375, ((0, 32),)),
        "cotangent": normal_values(splits[12], (MB, SEQS, LMAX, D), 1.0, 6.0, ((1, 32),)),
    }


eps = 1e-06
seq_group = 8

@jax.custom_vjp
def low(v):
    return lax.optimization_barrier(v.astype(jnp.bfloat16)).astype(jnp.float32)

@jax.custom_vjp
def low_back(v):
    return v

def low_keep(v):
    return (low(v), None)

def low_pass(kept, grad):
    return (grad,)

def back_keep(v):
    return (v, None)

def back_low(kept, grad):
    return (low(grad),)
low.defvjp(low_keep, low_pass)
low_back.defvjp(back_keep, back_low)

def matmul(left_side, right_side):
    return jnp.dot(left_side, right_side, precision=lax.Precision.HIGHEST)

def simple_norm(values):
    return values * lax.rsqrt(lax.optimization_barrier(jnp.mean(values * values, axis=-1, keepdims=True)) + eps)

def decay_of(decay_rates, length_rows):
    positions = jnp.arange(length_rows).astype(jnp.float32)
    distance = positions[:, None] - positions[None, :]
    return jnp.where(distance >= 0, jnp.exp(-decay_rates[:, None, None] * jnp.maximum(distance, 0.0)), 0.0)

def sequence_layer(weights, x_seq, seq_length, decay_rates):
    query_weight, key_weight, value_weight, gate_weight, out_weight, glu_left, glu_right, glu_down = weights
    length_rows = x_seq.shape[0]
    keep_mask = (jnp.arange(length_rows) < seq_length).astype(jnp.float32)[:, None]
    x_in = keep_mask * x_seq
    first_low = low(simple_norm(x_in))
    query_pre = low_back(matmul(first_low, query_weight))
    key_pre = low_back(matmul(first_low, key_weight))
    value_low = low(low_back(matmul(first_low, value_weight)))
    gate_up = low_back(matmul(first_low, gate_weight))
    head_shape = (length_rows, HEADS, HDIM)
    query_heads = low(jax.nn.silu(query_pre)).reshape(head_shape)
    key_heads = low(jax.nn.silu(key_pre)).reshape(head_shape)
    value_heads = value_low.reshape(head_shape)
    scores = low_back(jnp.einsum('thc,shc->hts', query_heads, key_heads, precision=lax.Precision.HIGHEST))
    weighted = low(scores * decay_of(decay_rates, length_rows))
    attention = low_back(jnp.einsum('hts,shc->thc', weighted, value_heads, precision=lax.Precision.HIGHEST))
    attention = attention.reshape(length_rows, HEADS * HDIM)
    gated_low = low(simple_norm(attention) * gate_up)
    hidden_res = x_in + low_back(matmul(gated_low, out_weight))
    third_low = low(simple_norm(hidden_res))
    left_part = low_back(matmul(third_low, glu_left))
    right_part = low_back(matmul(third_low, glu_right))
    product_low = low(left_part * right_part)
    return keep_mask * (hidden_res + low_back(matmul(product_low, glu_down)))

def pick_rows(source, row_index):
    return source[row_index]

def place_rows(values, row_index):
    return jnp.zeros_like(values).at[row_index].set(values)

def reference(tokens, lengths, deal_order, decay_rates, query_weight, key_weight, value_weight, gate_weight, out_weight, glu_left, glu_right, glu_down, cotangent):
    weights = tuple((weight.astype(jnp.float32) for weight in (query_weight, key_weight, value_weight, gate_weight, out_weight, glu_left, glu_right, glu_down)))
    micro_count, seq_count, length_rows, feature_count = tokens.shape
    dealt_tokens = jax.vmap(pick_rows)(tokens, deal_order).astype(jnp.float32)
    dealt_lengths = jax.vmap(pick_rows)(lengths, deal_order)
    group_count = micro_count * seq_count // seq_group
    group_tokens = dealt_tokens.reshape(group_count, seq_group, length_rows, feature_count)
    group_lengths = dealt_lengths.reshape(group_count, seq_group)
    group_cot = cotangent.astype(jnp.float32).reshape(group_count, seq_group, length_rows, feature_count)

    def scan_step(running, group_item):
        x_group, length_group, cot_group = group_item

        def forward(weight_set, x_set):

            def one_sequence(x_seq, seq_length):
                return sequence_layer(weight_set, x_seq, seq_length, decay_rates)
            return jax.vmap(one_sequence)(x_set, length_group)
        layer_out, pullback = jax.vjp(forward, weights, x_group)
        weight_grads, input_grads = pullback(cot_group)
        running = tuple((earlier + later for earlier, later in zip(running, weight_grads)))
        return (running, (layer_out, input_grads))
    zero_grads = tuple((jnp.zeros_like(weight) for weight in weights))
    totals, (outs_dealt, grads_dealt) = lax.scan(scan_step, zero_grads, (group_tokens, group_lengths, group_cot))
    shape_all = (micro_count, seq_count, length_rows, feature_count)
    layer_output = jax.vmap(place_rows)(outs_dealt.reshape(shape_all), deal_order).astype(jnp.bfloat16)
    input_grad = jax.vmap(place_rows)(grads_dealt.reshape(shape_all), deal_order).astype(jnp.bfloat16)
    return (layer_output, input_grad, totals[0], totals[1], totals[2], totals[3], totals[4], totals[5], totals[6], totals[7])
```

```python
import functools

import jax
import jax.numpy as jnp
from jax import lax
from jax.experimental import pallas as pl
from jax.experimental.pallas import tpu as pltpu
from jax.sharding import PartitionSpec as P

eps = 1e-06
axes = ("dp", "fsdp")
MESH = pl.DeviceIdType.MESH
ANY = pl.BlockSpec(memory_space=pl.ANY)


def times_weight(left_side, right_side):
    return jnp.dot(left_side, right_side, preferred_element_type=jnp.float32)


def outer_rows(left_side, right_side):
    return lax.dot_general(
        left_side, right_side, (((0,), (0,)), ((), ())), preferred_element_type=jnp.float32
    )


def times_transposed(left_side, right_side):
    return lax.dot_general(
        left_side, right_side, (((1,), (1,)), ((), ())), preferred_element_type=jnp.float32
    )


def simple_norm(values):
    factor = lax.rsqrt(jnp.mean(values * values, axis=-1, keepdims=True) + eps)
    return (values * factor, factor)


def norm_back(upstream, normed, factor):
    return factor * (upstream - normed * jnp.mean(upstream * normed, axis=-1, keepdims=True))


def silu_slope(values):
    sigmoid_value = jax.nn.sigmoid(values)
    return sigmoid_value * (1.0 + values * (1.0 - sigmoid_value))


def layer(x_rows, keep_mask, decay_table, heads, micro, weights, cot_rows):
    wq, wk, wv, wu, wo, wl, wr, wd = weights
    rows, features = x_rows.shape
    split = (micro, rows // micro, heads, features // heads)
    low = jnp.bfloat16
    x_in = keep_mask * x_rows.astype(jnp.float32)
    first_norm, first_factor = simple_norm(x_in)
    first_low = first_norm.astype(low)
    query_pre = times_weight(first_low, wq)
    key_pre = times_weight(first_low, wk)
    value = times_weight(first_low, wv).astype(low).reshape(split)
    gate_up = times_weight(first_low, wu)
    query = jax.nn.silu(query_pre).astype(low).reshape(split)
    key = jax.nn.silu(key_pre).astype(low).reshape(split)
    scores = jnp.einsum("bthc,bshc->bhts", query, key, preferred_element_type=jnp.float32)
    weighted = (scores * decay_table).astype(low)
    attention = jnp.einsum("bhts,bshc->bthc", weighted, value, preferred_element_type=jnp.float32)
    attention = attention.reshape(rows, features)
    second_norm, second_factor = simple_norm(attention)
    gated_low = (second_norm * gate_up).astype(low)
    hidden = x_in + times_weight(gated_low, wo)
    third_norm, third_factor = simple_norm(hidden)
    third_low = third_norm.astype(low)
    left_part = times_weight(third_low, wl)
    right_part = times_weight(third_low, wr)
    product_low = (left_part * right_part).astype(low)
    result = keep_mask * (hidden + times_weight(product_low, wd))

    back_out = keep_mask * cot_rows.astype(jnp.float32)
    back_out_low = back_out.astype(low)
    down_term = outer_rows(product_low, back_out_low)
    back_product = times_transposed(back_out_low, wd)
    back_left = (back_product * right_part).astype(low)
    back_right = (back_product * left_part).astype(low)
    left_term = outer_rows(third_low, back_left)
    right_term = outer_rows(third_low, back_right)
    back_third = times_transposed(back_left, wl) + times_transposed(back_right, wr)
    back_hidden = back_out + norm_back(back_third, third_norm, third_factor)
    back_branch = back_hidden.astype(low)
    out_term = outer_rows(gated_low, back_branch)
    back_gated = times_transposed(back_branch, wo)
    back_gate = (back_gated * second_norm).astype(low)
    back_attention = norm_back(back_gated * gate_up, second_norm, second_factor).astype(low)
    back_attention = back_attention.reshape(split)
    back_weighted = jnp.einsum(
        "bthc,bshc->bhts", back_attention, value, preferred_element_type=jnp.float32
    )
    back_value = jnp.einsum(
        "bhts,bthc->bshc", weighted, back_attention, preferred_element_type=jnp.float32
    )
    back_value = back_value.reshape(rows, features).astype(low)
    back_scores = (back_weighted * decay_table).astype(low)
    back_query = jnp.einsum("bhts,bshc->bthc", back_scores, key, preferred_element_type=jnp.float32)
    back_key = jnp.einsum("bhts,bthc->bshc", back_scores, query, preferred_element_type=jnp.float32)
    back_qpre = (back_query.reshape(rows, features) * silu_slope(query_pre)).astype(low)
    back_kpre = (back_key.reshape(rows, features) * silu_slope(key_pre)).astype(low)
    terms = (
        outer_rows(first_low, back_qpre),
        outer_rows(first_low, back_kpre),
        outer_rows(first_low, back_value),
        outer_rows(first_low, back_gate),
        out_term,
        left_term,
        right_term,
        down_term,
    )
    back_first = times_transposed(back_qpre, wq) + times_transposed(back_kpre, wk)
    back_first = (
        back_first + times_transposed(back_value, wv) + times_transposed(back_gate, wu)
    )
    back_input = keep_mask * (back_hidden + norm_back(back_first, first_norm, first_factor))
    return result.astype(low), back_input.astype(low), terms


def place():
    outer, inner = lax.axis_index("dp"), lax.axis_index("fsdp")
    return outer // 2, outer % 2, inner // 2, inner % 2


def at(x, c, z, y):
    return (x * 2 + c, z * 2 + y)


def copy_to(source, target, send, receive, device):
    return pltpu.make_async_remote_copy(
        src_ref=source,
        dst_ref=target,
        send_sem=send,
        recv_sem=receive,
        device_id=device,
        device_id_type=MESH,
    )


def meet_all(count, inner):
    me = lax.axis_index("dp") * inner + lax.axis_index("fsdp")
    barrier = pltpu.get_barrier_semaphore()

    @pl.loop(1, count)
    def _(k):
        other = (me + k) % count
        pl.semaphore_signal(
            barrier, inc=1, device_id=(other // inner, other % inner), device_id_type=MESH
        )

    pl.semaphore_wait(barrier, count - 1)
    return me


def halves(ref, half, size, first):
    lead = len(ref.shape) - 2
    return ref.at[(slice(None),) * lead + (pl.ds(first, size),)]


def keep_rows(keep, lengths, deal, me):
    for b in range(2):
        length = lengths[b, deal[b, me]]
        rows_at = lax.broadcasted_iota(jnp.int32, (256, 1), 0)
        keep[pl.ds(256 * b, 256)] = (rows_at < length).astype(jnp.float32)


def forward_kernel(
    tok, lengths, deal, rates, cot_h, sq, sk, sv, su, so, sl, sr, sd,
    ga, gl, gr, gd, x_o, n1_o, q_o, k_o, v_o, qp_o, kp_o, u_o, at_o, gt_o, h1_o, n3_o, lf_o, rt_o, res_o, pd_o,
    wa, wl, wr, wd, tk, td, xb, cb, n1, qb, kb, vb, qp, kp, ub, av, gt, h1, n3, pr_, lf, rst, pst, res, keep,
    own, tok_s, tok_r, zs, zr, ps, pr, qs, qr, cs, cr, ls, lr, out_s, st_s, in_s,
):
    low = jnp.bfloat16
    x, c, z, y = place()
    groups = 8

    def part(g, device, half=None):
        if g < 3:
            ref = wa.at[device, pl.ds(2 * g, 2 if g < 2 else 1)]
            return ref if half is None else halves(ref, half, 16, 16 * half)
        if g < 7:
            ref, first = (wl, wr)[(g - 3) // 2].at[device], 16 * ((g - 3) % 2)
            return ref.at[pl.ds(first, 16)] if half is None else ref.at[pl.ds(first + 8 * half, 8)]
        first, side = pl.multiple_of(device * 88, 8), pl.ds(512 * (g - 7), 512)
        if half is None:
            return wd.at[pl.ds(first, 88), side]
        return wd.at[pl.ds(first + 48 * half, 48 - 8 * half), side]

    def flat(xx, zz, yy):
        return (xx * 2 + c) * 8 + zz * 2 + yy

    me = lax.axis_index("dp") * 8 + lax.axis_index("fsdp")
    loads = [
        pltpu.make_async_copy(src, wa.at[me, i], own.at[i]) for i, src in enumerate((sq, sk, sv, su, so))
    ]
    loads += [
        pltpu.make_async_copy(sl, wl.at[me], own.at[5]),
        pltpu.make_async_copy(sr, wr.at[me], own.at[6]),
        pltpu.make_async_copy(sd, wd.at[pl.ds(pl.multiple_of(me * 88, 8), 88)], own.at[7]),
    ]
    small = [pltpu.make_async_copy(tok, tk, in_s.at[0]), pltpu.make_async_copy(cot_h, cb, in_s.at[1])]
    rows8 = pl.ds(pl.multiple_of(8 * me, 8), 8)
    mine = pltpu.make_async_copy(td.at[:, me], xb.at[:, rows8], own.at[8])

    def token(k):
        other = (me + k) % 32
        return copy_to(
            td.at[:, other], xb.at[:, rows8], tok_s.at[k], tok_r.at[k], (other // 8, other % 8)
        )

    def along_z(g, k):
        block = part(g, me)
        return copy_to(block, block, zs.at[g, k], zr.at[g, k], at(x, c, (z + k) % 4, y))

    def plane(g, k, way):
        block = part(g, flat(x, (z - k + 4) % 4, y))
        goal = at(1 - x, c, z, y) if way == 0 else at(x, c, z, 1 - y)
        return copy_to(block, block, ps.at[g, k, way], pr.at[g, k, way], goal)

    def relay(g, k, way):
        zz = (z - k + 4) % 4
        if way == 0:
            block, goal = part(g, flat(1 - x, zz, y), 0), at(x, c, z, 1 - y)
        else:
            block, goal = part(g, flat(x, zz, 1 - y), 1), at(1 - x, c, z, y)
        return copy_to(block, block, qs.at[g, k, way], qr.at[g, k, way], goal)

    def sibling(g, half):
        first = (half * 2 + c) * 8
        if g < 3:
            block = wa.at[pl.ds(first, 8), pl.ds(2 * g, 2 if g < 2 else 1)]
        elif g < 7:
            block = (wl, wr)[(g - 3) // 2].at[pl.ds(first, 8), pl.ds(16 * ((g - 3) % 2), 16)]
        else:
            block = wd.at[pl.ds(pl.multiple_of(first * 88, 8), 8 * 88), pl.ds(512 * (g - 7), 512)]
        return copy_to(block, block, cs.at[g, half], cr.at[g, half], at(x, 1 - c, z, y))

    def send_own(g):
        for way in range(2):
            plane(g, 0, way).start()

    def pass_own(g):
        for way in range(2):
            plane(g, 0, way).wait_recv()
            relay(g, 0, way).start()

    def send_z(g):
        for k in (2, 1, 3):
            along_z(g, k).start()

    def got_z(g):
        for k in range(1, 4):
            along_z(g, k).wait_recv()
            for way in range(2):
                plane(g, k, way).start()

    def got_plane(g):
        for k in range(1, 4):
            for way in range(2):
                plane(g, k, way).wait_recv()
                relay(g, k, way).start()

    def got_relay(g):
        for k in range(4):
            for way in range(2):
                relay(g, k, way).wait_recv()
        for half in range(2):
            sibling(g, half).start()

    def got_all(g):
        for half in range(2):
            sibling(g, half).wait_recv()

    def plane_z(k, xx):
        first = pl.multiple_of(flat(xx, z, 0) * 88, 8)
        block = wd.at[pl.ds(first, 176), pl.ds(512, 512)]
        return copy_to(block, block, ls.at[k, xx], lr.at[k, xx], at(x, c, (z + k) % 4, y))

    def last_z():
        for way in range(2):
            relay(groups, 0, way).wait_recv()
        for k in (2, 1, 3):
            for xx in range(2):
                plane_z(k, xx).start()

    def last_all():
        for k in range(1, 4):
            for xx in range(2):
                plane_z(k, xx).wait_recv()
        for half in range(2):
            sibling(groups, half).start()

    table = {
        "p": send_own, "r": pass_own, "z": send_z, "a": got_z, "b": got_plane, "c": got_relay, "d": got_all
    }

    def run(steps):
        for one in steps.split():
            table[one[0]](int(one[1]))

    outputs = []

    def give(source, target):
        one = pltpu.make_async_copy(source, target, out_s.at[len(outputs)])
        outputs.append(one)
        one.start()

    for one in loads + small:
        one.start()
    meet_all(32, 8)
    for one in loads:
        one.wait()
    run("z0 p0 p1 p2 p3")
    run("p4 p5 p6 p7 p8")
    for one in small:
        one.wait()

    @pl.loop(0, 32)
    def _(i):
        for b in range(2):
            td[b, i] = tk[b, deal[b, i]]

    @pl.loop(1, 32)
    def _(k):
        token(k).start()

    mine.start()
    run("z1")
    keep_rows(keep, lengths, deal, me)
    run("r0 r1 r2 r3")
    run("r4 r5 r6 r7 r8")
    run("a0 z2")
    mine.wait()

    @pl.loop(1, 32)
    def _(k):
        token(k).wait_recv()

    run("a1 z3 b0")
    give(xb, x_o)

    @pl.loop(0, 8)
    def _(i):
        r = pl.ds(64 * i, 64)
        x_in = xb[i // 4, pl.ds(64 * (i % 4), 64)].astype(jnp.float32) * keep[r]
        n1[r] = simple_norm(x_in)[0].astype(low)
        cb[i // 4, pl.ds(64 * (i % 4), 64)] = (
            cb[i // 4, pl.ds(64 * (i % 4), 64)].astype(jnp.float32) * keep[r]
        ).astype(low)

    give(n1, n1_o)
    run("a2 z4 b1 c0")
    run("a3 z5 b2 c1 d0")

    def columns(j):
        return pl.ds(pl.multiple_of(256 * j, 256), 256)

    def square(w, j):
        return wa[:, w, :, columns(j)].reshape(1024, 256)

    @pl.loop(0, 4)
    def _(j):
        for w, pre, full in ((0, qp, qb), (1, kp, kb)):
            value = times_weight(n1[...], square(w, j))
            pre[:, columns(j)] = value
            full[:, columns(j)] = (value / (1.0 + jnp.exp(-value))).astype(low)

    give(qp, qp_o)
    give(kp, kp_o)
    give(qb, q_o)
    give(kb, k_o)
    run("a4 z6 b3 c2 d1")

    @pl.loop(0, 4)
    def _(j):
        vb[:, columns(j)] = times_weight(n1[...], square(2, j)).astype(low)
        ub[:, columns(j)] = times_weight(n1[...], square(3, j))

    give(vb, v_o)
    give(ub, u_o)
    run("a5 z7 b4 c3")
    rows_at = lax.broadcasted_iota(jnp.int32, (256, 256), 0)
    columns_at = lax.broadcasted_iota(jnp.int32, (256, 256), 1)
    distance = (rows_at - columns_at).astype(jnp.float32)

    @pl.loop(0, 16)
    def _(i):
        r = pl.ds(pl.multiple_of(256 * (i // 8), 256), 256)
        h = pl.ds(pl.multiple_of(128 * (i % 8), 128), 128)
        scores = times_transposed(qb[r, h], kb[r, h])
        decay = jnp.where(distance >= 0, jnp.exp(-rates[i % 8] * jnp.maximum(distance, 0.0)), 0.0)
        weighted = (scores * decay).astype(low)
        av[r, h] = times_weight(weighted, vb[r, h])

    give(av, at_o)
    last_z()
    run("a6 b5 c4 d2")

    @pl.loop(0, 8)
    def _(i):
        r = pl.ds(64 * i, 64)
        gt[r] = (simple_norm(av[r])[0] * ub[r]).astype(low)

    give(gt, gt_o)

    @pl.loop(0, 4)
    def _(j):
        value = times_weight(gt[...], square(4, j))
        for b in range(2):
            r = pl.ds(256 * b, 256)
            h1[r, columns(j)] = xb[b, :, columns(j)].astype(jnp.float32) * keep[r] + value[256 * b : 256 * b + 256]

    give(h1, h1_o)

    @pl.loop(0, 8)
    def _(i):
        r = pl.ds(64 * i, 64)
        n3[r] = simple_norm(h1[r])[0].astype(low)

    give(n3, n3_o)
    give(wa, ga)
    run("a7 b6 c5")
    run("d3 d4")

    @pl.loop(0, 11)
    def _(j):
        lf[:, columns(j)] = times_weight(n3[...], wl[:, :, columns(j)].reshape(1024, 256))

    give(lf, lf_o)
    give(wl, gl)
    run("b7 c6")
    run("d5 d6")

    def store(j, which):
        slot = j % 2
        if which == 0:
            return pltpu.make_async_copy(rst.at[slot], rt_o.at[:, columns(j)], st_s.at[0, slot])
        return pltpu.make_async_copy(pst.at[slot], pd_o.at[columns(j)], st_s.at[1, slot])

    @pl.loop(0, 11)
    def _(j):
        @pl.when(j >= 2)
        def _():
            for which in range(2):
                store(j - 2, which).wait()

        slot = j % 2
        right = times_weight(n3[...], wr[:, :, columns(j)].reshape(1024, 256))
        rst[slot] = right
        product = (lf[:, columns(j)] * right).astype(low)
        pr_[:, columns(j)] = product
        pst[slot] = outer_rows(product, cb[...].reshape(512, 1024)).astype(low)
        for which in range(2):
            store(j, which).start()

        @pl.when(j == 4)
        def _():
            run("c7")

        @pl.when(j == 7)
        def _():
            last_all()

    give(wr, gr)
    for j in (9, 10):
        for which in range(2):
            store(j, which).wait()
    for side in range(2):
        run(("d7", "d8")[side])
        give(wd.at[:, pl.ds(512 * side, 512)], gd.at[:, pl.ds(512 * side, 512)])

        @pl.loop(2 * side, 2 * side + 2)
        def _(j):
            value = times_weight(pr_[...], wd[:, columns(j)])
            res[:, columns(j)] = ((h1[:, columns(j)] + value) * keep[...]).astype(low)

        give(res.at[:, pl.ds(512 * side, 512)], res_o.at[:, pl.ds(512 * side, 512)])
    for one in outputs:
        one.wait()

    @pl.loop(1, 32)
    def _(k):
        token(k).wait_send()

    for g in range(groups):
        for k in range(4):
            if k:
                along_z(g, k).wait_send()
            for way in range(2):
                plane(g, k, way).wait_send()
                relay(g, k, way).wait_send()
        for half in range(2):
            sibling(g, half).wait_send()
    for way in range(2):
        plane(groups, 0, way).wait_send()
        relay(groups, 0, way).wait_send()
    for half in range(2):
        sibling(groups, half).wait_send()
    for k in range(1, 4):
        for xx in range(2):
            plane_z(k, xx).wait_send()


def forward_all(tok, lengths, deal, rates, cot, *shards):
    low, full = jnp.bfloat16, jnp.float32
    dma = pltpu.SemaphoreType.DMA
    scalars = pl.BlockSpec(memory_space=pltpu.SMEM)
    wide = {"a": (32, 5, 32, 1024), "l": (32, 32, 2816), "d": (2816, 1024)}
    rows, ff, tokens = (512, 1024), (512, 2816), (2, 32, 8, 1024)
    outs = [(wide["a"], low), (wide["l"], low), (wide["l"], low), (wide["d"], low), ((2, 256, 1024), low)]
    outs += [(rows, low)] * 4 + [(rows, full)] * 4 + [(rows, low), (rows, full), (rows, low)]
    outs += [(ff, full), (ff, full), (rows, low), (wide["d"], low)]
    held = [(wide["a"], low), (wide["l"], low), (wide["l"], low), (wide["d"], low), (tokens, low), (tokens, low)]
    held += [((2, 256, 1024), low)] * 2 + [(rows, low)] * 4 + [(rows, full)] * 4
    held += [(rows, low), (rows, full), (rows, low), (ff, low)]
    held += [(ff, full), ((2, 512, 256), full), ((2, 256, 1024), low), (rows, low), ((512, 1), full)]
    g = 9
    sems = ((9,), (32,), (32,), (g, 4), (g, 4), (g, 4, 2), (g, 4, 2), (g, 4, 2), (g, 4, 2), (g, 2), (g, 2))
    sems += ((4, 2), (4, 2), (22,), (2, 2), (2,))
    return pl.pallas_call(
        forward_kernel,
        out_shape=[jax.ShapeDtypeStruct(*one) for one in outs],
        in_specs=[ANY] + [scalars] * 3 + [ANY] * 9,
        out_specs=[ANY] * len(outs),
        scratch_shapes=[pltpu.VMEM(*one) for one in held] + [dma(one) for one in sems],
        compiler_params=pltpu.CompilerParams(
            collective_id=0, has_side_effects=True, vmem_limit_bytes=62 * 1024 * 1024
        ),
        name="forward_all",
    )(tok, lengths, deal, rates, cot, *shards)


spans = ((0, 768), (768, 1024), (1792, 1024))


def backward_kernel(
    res, cot_h, lengths, deal, inverse, rates, ga, gl, gr, gd, x_h, n1_h, q_h, k_h, v_h, qp_h, kp_h, u_h, at_h, gt_h, h1_h, n3_h, lf_h, rt_h, pd,
    out_o, out_g, fa, fw, fd,
    ba, bw, bd, r0d, r1a, r1w, r1d, r2a, r2w, r2d, r3a, r3w, r3d, rz, rq, rp, ro, rg, tb, rb,
    dst, lst, rst, lfs, rts, cb, n3, acc, h1, bb, gt, qb, kb, vb, av, ub, n1, wst, keep,
    own, og_s, og_r, sz, tz, sq, tq, s0, t0, s1, t1, s2, t2, s3, t3, tile_s, tile_r, in_s, ff_s, wo_s, w_s, late_s, credit,
):
    low, full = jnp.bfloat16, jnp.float32
    x, c, z, y = place()
    me = meet_all(32, 8)
    kind = (2, 1, 1, 1, 0, 0, 0)
    base = [(ba, bw, bd)[i] for i in kind]
    got1 = [(r1a, r1w, r1d)[i] for i in kind]
    got2 = [(r2a, r2w, r2d)[i] for i in kind]
    got3 = [(r3a, r3w, r3d)[i] for i in kind]
    slots = 3

    def own_half(xx):
        return pltpu.make_async_copy(pd.at[xx, c], bd.at[xx], own.at[xx])

    down = (pl.ds(0, 48), pl.ds(48, 40))

    def stage0(which, xx):
        rows = (slice(None), slice(None), down[which])
        return copy_to(
            pd.at[(xx, 1 - c) + rows],
            r0d.at[(xx,) + rows],
            s0.at[which, xx],
            t0.at[which, xx],
            at(x, 1 - c, z, y),
        )

    def inner(g, half=None):
        if g == 0:
            return (down[0] if half is None else pl.ds(24 * half, 24),)
        if g < 4:
            return (slice(None) if half is None else half, slice(None), pl.ds(*spans[g - 1]))
        if g == 4:
            return (4,) if half is None else (4, pl.ds(16 * half, 16))
        return (pl.ds(2 * (g - 5), 2),) if half is None else (2 * (g - 5) + half,)

    def stage1(g, half):
        every, rest = slice(None), inner(g, half)
        if half == 0:
            return [
                copy_to(
                    base[g].at[(1 - x, every, every) + rest],
                    got1[g].at[(0, every, every) + rest],
                    s1.at[g, 0],
                    t1.at[g, 0],
                    at(1 - x, c, z, y),
                )
            ]
        return [
            copy_to(
                base[g].at[(xx, every, 1 - y) + rest],
                got1[g].at[(0, every, xx) + rest],
                s1.at[g, 1 + xx],
                t1.at[g, 1 + xx],
                at(x, c, z, 1 - y),
            )
            for xx in range(2)
        ]

    def stage2(g, half):
        every, rest = slice(None), inner(g, half)
        if half == 0:
            source, goal = base[g].at[(x, every, 1 - y) + rest], at(x, c, z, 1 - y)
        else:
            source, goal = base[g].at[(1 - x, every, y) + rest], at(1 - x, c, z, y)
        return copy_to(
            source, got2[g].at[(every,) + rest], s2.at[g, half], t2.at[g, half], goal
        )

    def stage3(g, k):
        zz = (z + k) % 4
        rest = inner(g)
        return copy_to(
            base[g].at[(x, zz, y) + rest],
            got3[g].at[(k - 1,) + rest],
            s3.at[g, k - 1],
            t3.at[g, k - 1],
            at(x, c, zz, y),
        )

    sends = ((res, ro), (cb, rg))

    def send_out(k, which):
        other = (me + k) % 32
        source, target = sends[which]
        return copy_to(
            source.at[:, pl.ds(pl.multiple_of(8 * other, 8), 8)],
            target.at[:, me],
            og_s.at[which, k],
            og_r.at[which, k],
            (other // 8, other % 8),
        )

    def send_own(which):
        source, target = sends[which]
        return pltpu.make_async_copy(
            source.at[:, pl.ds(pl.multiple_of(8 * me, 8), 8)], target.at[:, me], own.at[2 + which]
        )

    def add_into(ref, index, other, other_index):
        ref[index] = (ref[index].astype(full) + other[other_index].astype(full)).astype(low)

    def start1(g):
        for half in range(2):
            for one in stage1(g, half):
                one.start()

    def work0(which):
        for xx in range(2):
            if which == 0:
                own_half(xx).wait()
            stage0(which, xx).wait_recv()

            @pl.loop(0, 8)
            def _(i):
                where = (xx, i // 2, i % 2, down[which])
                add_into(bd, where, r0d, where)

        if which == 0:
            start1(0)

    def down_z(k):
        zz = (z + k) % 4
        return copy_to(
            bd.at[:, zz, :, down[1]], rz.at[k - 1], sz.at[k - 1], tz.at[k - 1], at(x, c, zz, y)
        )

    top, bottom = pl.ds(48, 24), pl.ds(72, 16)

    def down_plane(step, half):
        every = slice(None)
        if step == 0 and half == 0:
            source, target, goal = bd.at[1 - x, z, :, top], rq.at[:, pl.ds(0, 24)], at(1 - x, c, z, y)
        elif step == 0:
            source, target, goal = bd.at[:, z, 1 - y, bottom], rq.at[:, pl.ds(24, 16)], at(x, c, z, 1 - y)
        elif half == 0:
            source, target, goal = bd.at[x, z, 1 - y, top], rp.at[pl.ds(0, 24)], at(x, c, z, 1 - y)
        else:
            source, target, goal = bd.at[1 - x, z, y, bottom], rp.at[pl.ds(24, 16)], at(1 - x, c, z, y)
        return copy_to(source, target, sq.at[step, half], tq.at[step, half], goal)

    def down_z_start():
        for k in range(1, 4):
            down_z(k).start()

    def down_z_take():
        for k in range(1, 4):
            down_z(k).wait_recv()

        @pl.loop(0, 4)
        def _(i):
            where = (i // 2, z, i % 2, down[1])
            total = bd[where].astype(full)
            for k in range(3):
                total = total + rz[k, i // 2, i % 2].astype(full)
            bd[where] = total.astype(low)

        for half in range(2):
            down_plane(0, half).start()

    def down_plane_take():
        down_plane(0, 0).wait_recv()
        for i in range(2):
            add_into(bd, (x, z, i, top), rq, (i, pl.ds(0, 24)))
        down_plane(1, 0).start()
        down_plane(0, 1).wait_recv()
        for i in range(2):
            add_into(bd, (i, z, y, bottom), rq, (i, pl.ds(24, 16)))
        down_plane(1, 1).start()

    def down_last():
        for half in range(2):
            down_plane(1, half).wait_recv()
        fd[down[1]] = bd[x, z, y, down[1]].astype(full) + rp[...].astype(full)

    def work1(g):
        for half in range(2):
            for one in stage1(g, half):
                one.wait_recv()

            @pl.loop(0, 8)
            def _(i):
                r = inner(g, half)
                where = (x, i // 2, i % 2) if half == 0 else (i % 2, i // 2, y)
                add_into(base[g], where + r, got1[g], (0, i // 2, i % 2) + r)

            stage2(g, half).start()

    def work2(g):
        for half in range(2):
            stage2(g, half).wait_recv()

            @pl.loop(0, 4)
            def _(i):
                r = inner(g, half)
                add_into(base[g], (x, i, y) + r, got2[g], (i,) + r)

        for k in range(1, 4):
            stage3(g, k).start()

    def work3(g):
        for k in range(1, 4):
            stage3(g, k).wait_recv()
        if g == 0:
            parts = [((down[0],), fd, (down[0],))]
        elif g < 4:
            parts = [(((i, slice(None), pl.ds(*spans[g - 1])),) + (fw, (i, slice(None), pl.ds(*spans[g - 1])))) for i in range(2)]
        elif g == 4:
            parts = [((4,), fa, (4,))]
        else:
            parts = [((2 * (g - 5) + i,), fa, (2 * (g - 5) + i,)) for i in range(2)]
        for rest, goal, where in parts:
            total = base[g][(x, z, y) + rest].astype(full)
            for k in range(3):
                total = total + got3[g][(k,) + rest].astype(full)
            goal[where] = total

    def tile_send(t):
        slot = t % slots
        return copy_to(
            tb.at[slot, :, :, 1 - c], rb.at[slot], tile_s.at[slot], tile_r.at[slot], at(x, 1 - c, z, y)
        )

    def tile_pair(t, first, second):
        slot = t % slots

        @pl.when(t >= slots)
        def _():
            pl.semaphore_wait(credit, 1)

        tb[slot, 0] = first.astype(low).reshape(2, 2, 4, 2, 32, 256)
        tb[slot, 1] = second.astype(low).reshape(2, 2, 4, 2, 32, 256)
        tile_send(t).start()

    def tile_take(t, targets):
        slot = t % slots
        tile_send(t).wait()
        for i, (ref, index) in enumerate(targets):
            for xx in range(2):
                ref[(xx,) + index] = (
                    tb[slot, i, xx, c].astype(full) + rb[slot, i, xx].astype(full)
                ).astype(low)
        pl.semaphore_signal(credit, inc=1, device_id=at(x, 1 - c, z, y), device_id_type=MESH)

    def columns(j, size=256):
        return pl.ds(pl.multiple_of(size * j, size), size)

    every = slice(None)

    def load(i, source, target):
        return pltpu.make_async_copy(source, target, in_s.at[i])

    early = [
        load(i, *one)
        for i, one in enumerate(((cot_h, cb), (n3_h, n3), (h1_h, h1)))
    ]
    later = [
        load(4 + i, *one)
        for i, one in enumerate(
            ((gt_h, gt), (at_h, av), (u_h, ub), (q_h, qb), (k_h, kb), (v_h, vb), (n1_h, n1))
        )
    ]

    def ff_loads(f):
        slot = f % 2
        pairs = (
            (gd.at[pl.ds(8 * f, 8)], dst),
            (gl.at[:, :, columns(f)], lst),
            (gr.at[:, :, columns(f)], rst),
            (lf_h.at[:, columns(f)], lfs),
            (rt_h.at[:, columns(f)], rts),
        )
        return [
            pltpu.make_async_copy(source, target.at[slot], ff_s.at[i, slot])
            for i, (source, target) in enumerate(pairs)
        ]

    for one in early:
        one.start()
    for one in ff_loads(0):
        one.start()
    send_own(0).start()

    @pl.loop(1, 32)
    def _(k):
        send_out(k, 0).start()

    for xx in range(2):
        stage0(0, xx).start()
        own_half(xx).start()

    for one in later:
        one.start()
    keep_rows(keep, lengths, deal, me)
    for one in early:
        one.wait()

    @pl.loop(0, 8)
    def _(i):
        r = pl.ds(64 * (i % 4), 64)
        cb[i // 4, r] = (cb[i // 4, r].astype(full) * keep[pl.ds(64 * i, 64)]).astype(low)

    @pl.loop(0, 11)
    def _(f):
        slot = f % 2

        @pl.when(f < 10)
        def _():
            for one in ff_loads(f + 1):
                one.start()

        for one in ff_loads(f):
            one.wait()
        back_product = times_transposed(cb[...].reshape(512, 1024), dst[slot].reshape(256, 1024))
        back_left = (back_product * rts[slot]).astype(low)
        back_right = (back_product * lfs[slot]).astype(low)
        value = times_transposed(back_left, lst[slot].reshape(1024, 256)) + times_transposed(
            back_right, rst[slot].reshape(1024, 256)
        )

        @pl.when(f == 0)
        def _():
            acc[...] = value

        @pl.when(f > 0)
        def _():
            acc[...] += value

        tile_pair(f, outer_rows(n3[...].reshape(512, 1024), back_left), outer_rows(n3[...].reshape(512, 1024), back_right))

        @pl.when(f >= 1)
        def _():
            tile_take(f - 1, [(bw, (every, every, i, every, columns(f - 1))) for i in range(2)])

        @pl.when(f == 0)
        def _():
            for xx in range(2):
                stage0(1, xx).start()

        @pl.when(f == 1)
        def _():
            work0(0)

        @pl.when(f == 3)
        def _():
            start1(1)

        @pl.when(f == 4)
        def _():
            work0(1)
            down_z_start()
            work1(0)

        @pl.when(f == 6)
        def _():
            work1(1)

        @pl.when(f == 7)
        def _():
            start1(2)

    tile_take(10, [(bw, (every, every, i, every, columns(10))) for i in range(2)])
    start1(3)

    def wo_load(i):
        return pltpu.make_async_copy(ga.at[pl.ds(8 * i, 8), 4], dst.at[i % 2], wo_s.at[i % 2])

    def w_load(i):
        return pltpu.make_async_copy(ga.at[pl.ds(4 * i, 4), pl.ds(0, 4)], wst.at[i % 2], w_s.at[i % 2])

    x_load = load(11, x_h, n3)
    x_load.start()
    wo_load(0).start()
    w_load(0).start()

    @pl.loop(0, 8)
    def _(i):
        r = pl.ds(64 * i, 64)
        normed, factor = simple_norm(h1[r])
        hidden = cb[i // 4, pl.ds(64 * (i % 4), 64)].astype(full) + norm_back(acc[r], normed, factor)
        h1[r] = hidden
        bb[r] = hidden.astype(low)

    work2(1)
    work1(2)
    for one in later:
        one.wait()

    def out_where(t):
        return [(ba, (every, every, 4, every, columns(2 * (t - 11) + i))) for i in range(2)]

    @pl.loop(11, 13)
    def _(t):
        j = t - 11
        tile_pair(
            t,
            outer_rows(gt[...], bb[:, columns(2 * j)]),
            outer_rows(gt[...], bb[:, columns(2 * j + 1)]),
        )

        @pl.when(t > 11)
        def _():
            tile_take(t - 1, out_where(t - 1))

    @pl.loop(0, 4)
    def _(i):
        @pl.when(i < 3)
        def _():
            wo_load(i + 1).start()

        wo_load(i).wait()
        acc[:, columns(i)] = times_transposed(bb[...], dst[i % 2].reshape(256, 1024))

    tile_take(12, out_where(12))
    work2(0)

    @pl.loop(0, 8)
    def _(i):
        r = pl.ds(64 * i, 64)
        normed, factor = simple_norm(av[r])
        back_gated = acc[r]
        gt[r] = (back_gated * normed).astype(low)
        bb[r] = norm_back(back_gated * ub[r], normed, factor).astype(low)

    pres = [pltpu.make_async_copy(qp_h, acc, late_s.at[0]), pltpu.make_async_copy(kp_h, av, late_s.at[1])]
    for one in pres:
        one.start()
    for one in pres:
        one.wait()
    rows_at = lax.broadcasted_iota(jnp.int32, (256, 256), 0)
    columns_at = lax.broadcasted_iota(jnp.int32, (256, 256), 1)
    distance = (rows_at - columns_at).astype(full)

    @pl.loop(0, 16)
    def _(i):
        r = pl.ds(pl.multiple_of(256 * (i // 8), 256), 256)
        h = columns(i % 8, 128)
        decay = jnp.where(distance >= 0, jnp.exp(-rates[i % 8] * jnp.maximum(distance, 0.0)), 0.0)
        query, key, value, above = qb[r, h], kb[r, h], vb[r, h], bb[r, h]
        weighted = (times_transposed(query, key) * decay).astype(low)
        back_scores = (times_transposed(above, value) * decay).astype(low)
        vb[r, h] = outer_rows(weighted, above).astype(low)
        qb[r, h] = (times_weight(back_scores, key) * silu_slope(acc[r, h])).astype(low)
        kb[r, h] = (outer_rows(back_scores, query) * silu_slope(av[r, h])).astype(low)

        @pl.when(i == 5)
        def _():
            start1(4)

        @pl.when(i == 10)
        def _():
            work2(2)

        @pl.when(i == 11)
        def _():
            work1(3)

        @pl.when(i == 13)
        def _():
            work1(4)

    def square_where(t):
        return lambda pair: [
            (ba, (every, every, 2 * pair + i, every, columns((t - 13) % 4))) for i in range(2)
        ]

    for pair, (first, second) in enumerate(((qb, kb), (vb, gt))):
        begin = 13 + 4 * pair

        @pl.loop(begin, begin + 4)
        def _(t):
            j = columns(t - begin)
            tile_pair(t, outer_rows(n1[...], first[:, j]), outer_rows(n1[...], second[:, j]))

            @pl.when(t > begin)
            def _():
                tile_take(t - 1, square_where(t - 1)(pair))

        tile_take(begin + 3, square_where(begin + 3)(pair))
        start1(5 + pair)
        if pair == 0:
            work2(3)
    work3(2)
    down_z_take()
    work2(4)
    work3(0)

    @pl.loop(0, 8)
    def _(i):
        @pl.when(i < 7)
        def _():
            w_load(i + 1).start()

        w_load(i).wait()
        value = None
        for w, ref in enumerate((qb, kb, vb, gt)):
            one = times_transposed(ref[...], wst[i % 2, :, w].reshape(128, 1024))
            value = one if value is None else value + one
        acc[:, columns(i, 128)] = value

    x_load.wait()

    @pl.loop(0, 8)
    def _(i):
        r, half = pl.ds(64 * i, 64), (i // 4, pl.ds(64 * (i % 4), 64))
        normed, factor = simple_norm(n3[half].astype(full) * keep[r])
        cb[half] = (keep[r] * (h1[r] + norm_back(acc[r], normed, factor))).astype(low)

    def arrived(which):
        send_own(which).wait()

        @pl.loop(1, 32)
        def _(k):
            send_out(k, which).wait()

        held, staged, goal = ((ro, n3, out_o), (rg, n1, out_g))[which]

        @pl.loop(0, 32)
        def _(i):
            for b in range(2):
                value = held[b, inverse[b, i]]
                if which == 0:
                    staged[b, pl.ds(pl.multiple_of(8 * i, 8), 8)] = value
                else:
                    staged[pl.ds(pl.multiple_of(256 * b + 8 * i, 8), 8)] = value

        return pltpu.make_async_copy(staged, goal, in_s.at[which])

    work1(5)
    work3(3)
    send_own(1).start()

    @pl.loop(1, 32)
    def _(k):
        send_out(k, 1).start()

    given = arrived(0)
    given.start()
    work2(5)
    work3(4)
    down_plane_take()
    work1(6)
    work2(6)
    down_last()
    work3(1)
    given.wait()
    given = arrived(1)
    given.start()
    work3(5)
    work3(6)
    given.wait()
    for which in range(2):
        for xx in range(2):
            stage0(which, xx).wait_send()
    for k in range(1, 4):
        down_z(k).wait_send()
    for half in range(2):
        for step in range(2):
            down_plane(step, half).wait_send()
    for g in range(7):
        for half in range(2):
            for one in stage1(g, half):
                one.wait_send()
            stage2(g, half).wait_send()
        for k in range(1, 4):
            stage3(g, k).wait_send()
    pl.semaphore_wait(credit, slots)


def backward_all(res, cot, lengths, deal, inverse, rates, *held):
    low, full = jnp.bfloat16, jnp.float32
    dma = pltpu.SemaphoreType.DMA
    whole = pl.BlockSpec(memory_space=pltpu.VMEM)
    scalars = pl.BlockSpec(memory_space=pltpu.SMEM)
    tails = ((5, 32, 1024), (2, 32, 2816), (88, 1024))
    rows = (512, 1024)
    bufs = [pltpu.VMEM((2, 4, 2) + tail, low) for tail in tails] + [pltpu.VMEM((2, 4, 2, 88, 1024), low)]
    for lead in ((1, 4, 2), (4,), (3,)):
        bufs += [pltpu.VMEM(lead + tail, low) for tail in tails[:2] + ((48, 1024),)]
    bufs += [pltpu.VMEM((3, 2, 2, 40, 1024), low), pltpu.VMEM((2, 40, 1024), low), pltpu.VMEM((40, 1024), low)]
    bufs += [pltpu.VMEM((2, 32, 8, 1024), low)] * 2
    bufs += [pltpu.VMEM((3, 2, 2, 2, 4, 2, 32, 256), low), pltpu.VMEM((3, 2, 2, 4, 2, 32, 256), low)]
    bufs += [pltpu.VMEM((2, 8, 32, 1024), low)] + [pltpu.VMEM((2, 32, 32, 256), low)] * 2
    bufs += [pltpu.VMEM((2, 512, 256), full)] * 2
    bufs += [pltpu.VMEM((2, 256, 1024), low)] * 2 + [pltpu.VMEM(rows, full)] * 2
    bufs += [pltpu.VMEM(rows, low)] * 5 + [pltpu.VMEM(rows, full)] * 2
    bufs += [pltpu.VMEM(rows, low)]
    bufs += [pltpu.VMEM((2, 4, 4, 32, 1024), low), pltpu.VMEM((512, 1), full)]
    sems = ((4,), (2, 32), (2, 32), (3,), (3,), (2, 2), (2, 2), (2, 2), (2, 2), (7, 3), (7, 3), (7, 2), (7, 2), (7, 3), (7, 3))
    sems += ((3,), (3,), (12,), (5, 2), (2,), (2,), (2,))
    return pl.pallas_call(
        backward_kernel,
        out_shape=(
            jax.ShapeDtypeStruct((2, 256, 1024), low),
            jax.ShapeDtypeStruct(rows, low),
        )
        + tuple(jax.ShapeDtypeStruct(tail, full) for tail in tails),
        in_specs=[ANY] * 2 + [scalars] * 4 + [ANY] * len(held),
        out_specs=(ANY, ANY) + (whole,) * 3,
        scratch_shapes=bufs + [dma(one) for one in sems] + [pltpu.SemaphoreType.REGULAR],
        compiler_params=pltpu.CompilerParams(
            collective_id=1, has_side_effects=True, vmem_limit_bytes=63 * 1024 * 1024
        ),
        name="backward_all",
    )(res, cot, lengths, deal, inverse, rates, *held)


def common(tokens, lengths, deal_order, decay_rates):
    slot = lax.axis_index(axes)
    positions = jnp.arange(tokens[0], dtype=jnp.float32)
    distance = positions[:, None] - positions[None, :]
    decay_table = jnp.where(
        distance >= 0, jnp.exp(-decay_rates[:, None, None] * jnp.maximum(distance, 0.0)), 0.0
    )
    mine = lax.dynamic_index_in_dim(deal_order, slot, 1, keepdims=True)
    length = jnp.take_along_axis(lengths, mine, axis=1)
    keep = (jnp.arange(tokens[0])[None, :] < length).astype(jnp.float32)
    return decay_table, keep.reshape(-1, 1)


def by_collectives(tokens, lengths, deal_order, decay_rates, *rest):
    shards, cotangent = rest[:8], rest[8]
    micro, _, _, features = tokens.shape
    rows = cotangent.shape[2]
    dealt = jax.vmap(lambda t, o: jnp.take(t, o, axis=0))(tokens, deal_order)
    arrived = lax.all_to_all(dealt, axes, split_axis=1, concat_axis=2, tiled=True)
    decay_table, keep = common((rows,), lengths, deal_order, decay_rates)
    weights = tuple(lax.all_gather(one, axes, axis=0, tiled=True) for one in shards)
    result, back_input, terms = layer(
        arrived.reshape(micro * rows, features),
        keep,
        decay_table,
        decay_rates.shape[0],
        micro,
        weights,
        cotangent.reshape(micro * rows, features),
    )

    def back(values):
        values = values.reshape(micro, 1, rows, features)
        spread = lax.all_to_all(values, axes, split_axis=2, concat_axis=1, tiled=True)
        return jax.vmap(lambda v, o: jnp.zeros_like(v).at[o].set(v))(spread, deal_order)

    owned = tuple(lax.psum_scatter(one, axes, scatter_dimension=0, tiled=True) for one in terms)
    return (back(result), back(back_input)) + owned


def hand_out(*given):
    counts = (1, 1, 5, 2, 1)
    sources, total = len(given), sum(counts)

    def kernel(*refs):
        held = refs[sources + total : 2 * sources + total]
        into, out = refs[-2:]
        loads = [pltpu.make_async_copy(refs[i], held[i], into.at[i]) for i in range(sources)]
        pieces = [one.at[i] if n > 1 else one for one, n in zip(held, counts) for i in range(n)]
        stores = [
            pltpu.make_async_copy(*pair, out.at[i])
            for i, pair in enumerate(zip(pieces, refs[sources : sources + total]))
        ]
        for one in loads:
            one.start()
        first = 0
        for load, n in zip(loads, counts):
            load.wait()
            for one in stores[first : first + n]:
                one.start()
            first += n
        for one in stores:
            one.wait()

    shapes = []
    for one, n in zip(given, counts):
        shapes += [jax.ShapeDtypeStruct(one.shape if n == 1 else one.shape[1:], one.dtype)] * n
    return pl.pallas_call(
        kernel,
        out_shape=shapes,
        in_specs=[ANY] * sources,
        out_specs=[ANY] * total,
        scratch_shapes=[pltpu.VMEM(one.shape, one.dtype) for one in given]
        + [pltpu.SemaphoreType.DMA((sources,)), pltpu.SemaphoreType.DMA((total,))],
        name="hand_out",
    )(*given)


def by_kernels(tokens, lengths, deal_order, decay_rates, *rest):
    shards, cotangent = rest[:8], rest[8]
    micro, count, _, features = tokens.shape
    rows = cotangent.shape[2]
    cot = cotangent.reshape(micro, rows, features)
    *saved, result, pd = forward_all(tokens, lengths, deal_order, decay_rates, cot, *shards)
    saved[3] = saved[3].reshape(-1, 32, features)
    saved[15] = saved[15].reshape(micro, rows, features)
    slots = jnp.arange(count, dtype=jnp.int32)
    inverse = jnp.sum(
        jnp.where(deal_order[:, :, None] == slots[None, None, :], slots[None, :, None], 0), axis=1
    )
    result, back_input, fa, fw, fd = backward_all(
        result.reshape(micro, rows, features),
        cot,
        lengths,
        deal_order,
        inverse,
        decay_rates,
        *saved,
        pd.reshape(2, 2, 4, 2, 88, features),
    )
    shape = tokens.shape
    return tuple(hand_out(result.reshape(shape), back_input.reshape(shape), fa, fw, fd))


def solution(mesh):
    rows = P(axes, None)
    blocks = P(None, None, axes, None)
    kernels = mesh.shape["dp"] == 4 and mesh.shape["fsdp"] == 8
    return jax.shard_map(
        by_kernels if kernels else by_collectives,
        mesh=mesh,
        in_specs=(blocks, P(), P(), P()) + (rows,) * 8 + (P(None, axes, None, None),),
        out_specs=(blocks, blocks) + (rows,) * 8,
        check_vma=False,
    )
```
